256 devices in a mesh: hop: 16 (over y, z_lo), tensor: 16 (over x, z_hi, core).
Axes of the slice: x: 4, y: 4, z: 8 (z_hi: 2, z_lo: 4; z = z_hi * 4 + z_lo), core: 2. Of those that a mesh axis runs over, the one named last changes fastest.
Arguments:
- tokens: bfloat16 [3, 4096, 1024], P(None, 'hop', 'tensor'), may hold values from -17 to 17
- targets: bfloat16 [2, 4096, 1024], P(None, 'hop', 'tensor'), may hold values from -6 to 6
- w_in: bfloat16 [16, 1024, 32768], P('hop', None, 'tensor'), may hold values from -0.1875 to 0.1875
- w_out: bfloat16 [32768, 1024], P('tensor', 'hop'), may hold values from -0.03125 to 0.03125
- noise_field: bfloat16 [16, 1024, 32768], P('hop', None, 'tensor'), may hold values from -18 to 18
- step_size: float32 [16], replicated, may hold values from 0.005 to 0.02
- clip_ratio: float32 [16], replicated, may hold values from 0.5 to 2
- noise_mult: float32 [16], replicated, may hold values from 0.002 to 0.02
- plan: int32 [16], replicated, may hold values from 0 to 15, each once
- live_rows: int32 [2, 16], P(None, 'hop'), may hold values from 128 to 256
Outputs:
- predictions: bfloat16 [4096, 1024], P('hop', 'tensor')
- row_losses: float32 [2, 4096], P(None, 'hop')
The draws below stay inside these ranges and needn't reach their ends.
Inputs may be any that keep to these rules, and one draw needn't show every extreme that they name: `plan`: each configuration names the partition that holds it in round two; every partition is named once. The first live_rows[k, g] rows of partition g are live in round k.
All inputs are finite; a program needn't handle non-finite values.
Results may differ from the reference program's by a relative error of at most 0.0085.
Values may be sent and summed in bfloat16 or wider, within the bound.
No kernel may reach another device: no remote copies, remote signals or barrier semaphores. Data moves between devices by JAX's collectives and lax.ppermute only.
A program may use at most 128 MiB of HBM per device.

```python
import math
import jax
import jax.numpy as jnp
from jax import lax

D = 1024
FF = 32768
ROWS = 256
CONFIGS = 16
ALL_ROWS = 4096


def draw_tokens(key, part):
    first_key, second_key = jax.random.split(jax.random.fold_in(key, 11))
    entries = jnp.clip(jax.random.normal(first_key, (3, ALL_ROWS, D), jnp.float32), -5.0, 5.0)
    scales = jnp.exp(jax.random.uniform(second_key, (3, ALL_ROWS, 1), jnp.float32, math.log(0.33), math.log(3.3)))
    return (entries * scales).astype(jnp.bfloat16)


def draw_noise_field(key, part):
    first_key = jax.random.fold_in(key, 23)
    columns = jnp.arange(FF, dtype=jnp.float32) / FF
    entries = jnp.clip(jax.random.normal(first_key, (CONFIGS, D, FF), jnp.float32), -5.0, 5.0)
    scales = jnp.power(3.0, columns)[None, None, :]
    return (entries * scales).astype(jnp.bfloat16)


def plant(values, rng, least, top_value):
    index_at = [jax.random.randint(jax.random.fold_in(rng, axis), (), 0, length) for axis, length in enumerate(values.shape)]
    widest = values.shape.index(max(values.shape))
    beside = index_at[:widest] + [(index_at[widest] + 1) % values.shape[widest]] + index_at[widest + 1:]
    return values.at[tuple(index_at)].set(least).at[tuple(beside)].set(top_value)


def shard_levels(stream_key, extent, cuts, low, top_value):
    level = 1.0
    for position, blocks in cuts:
        draws = jax.random.uniform(jax.random.fold_in(jax.random.fold_in(stream_key, 6), position), (blocks,), jnp.float32, low / len(cuts), top_value / len(cuts))
        level = level * jnp.repeat(jnp.exp(draws), extent[position] // blocks).reshape((-1,) + (1,) * (len(extent) - 1 - position))
    return level


def normal_values(stream_key, shape, scale, most, cuts=(), kind=jnp.bfloat16):
    values = scale * jax.random.normal(stream_key, shape, jnp.float32)
    if cuts:
        values = values * shard_levels(stream_key, shape, cuts, -0.22, 0.18)
    return jnp.clip(values, -most, most).astype(kind)


def setup_inputs(seed: int = 0) -> dict:
    keys = jax.random.split(jax.random.key(seed), 11)
    return {
        "tokens": draw_tokens(jax.random.fold_in(keys[10], 71), 0),
        "targets": normal_values(keys[1], (2, ALL_ROWS, D), 1.0, 6.0, ((1, 16), (2, 16))),
        "w_in": normal_values(keys[2], (CONFIGS, D, FF), D ** -0.5, 0.1875, ((0, 16), (2, 16))),
        "w_out": normal_values(keys[3], (FF, D), FF ** -0.5, 0.03125, ((0, 16), (1, 16))),
        "noise_field": draw_noise_field(jax.random.fold_in(keys[10], 71), 0),
        "step_size": jnp.clip(jnp.exp(jax.random.uniform(keys[5], (CONFIGS,), jnp.float32, math.log(0.005), math.log(0.02))), 0.005, 0.02),
        "clip_ratio": jnp.clip(jnp.exp(jax.random.uniform(keys[6], (CONFIGS,), jnp.float32, math.log(0.5), math.log(2.0))), 0.5, 2.0),
        "noise_mult": jnp.clip(jnp.exp(jax.random.uniform(keys[7], (CONFIGS,), jnp.float32, math.log(0.002), math.log(0.02))), 0.002, 0.02),
        "plan": jax.random.permutation(keys[8], CONFIGS).astype(jnp.int32),
        "live_rows": plant(jax.random.randint(keys[9], (2, CONFIGS), ROWS // 2, ROWS + 1), jax.random.fold_in(keys[9], 1), ROWS // 2, ROWS).astype(jnp.int32),
    }


def gelu_parts(pre_act):
    inside = 0.7978845608 * (pre_act + 0.044715 * pre_act * pre_act * pre_act)
    tangent = jnp.tanh(inside)
    output = 0.5 * pre_act * (1.0 + tangent)
    slope_value = 0.5 * (1.0 + tangent) + 0.5 * pre_act * (1.0 - tangent * tangent) * 0.7978845608 * (1.0 + 0.134145 * pre_act * pre_act)
    return (output, slope_value)

def train_round(weights, inputs, wanted, noise_block, live_count, learn_rate, clip_share, noise_scale, w_out):
    pre_act = jnp.dot(inputs, weights, preferred_element_type=jnp.float32)
    output, slope_value = gelu_parts(pre_act)
    active = output.astype(jnp.bfloat16)
    result = jnp.dot(active, w_out, preferred_element_type=jnp.float32)
    differ = result - wanted.astype(jnp.float32)
    live_mask = (jnp.arange(inputs.shape[0], dtype=jnp.int32) < live_count).astype(jnp.float32)
    losses = 0.5 * lax.optimization_barrier(jnp.sum(differ * differ, axis=1)) * live_mask
    backed = differ.astype(jnp.bfloat16)
    grad_act = jnp.dot(backed, w_out.T, preferred_element_type=jnp.float32) * slope_value
    input_square = lax.optimization_barrier(jnp.sum(jnp.square(inputs.astype(jnp.float32)), axis=1))
    grad_square = lax.optimization_barrier(jnp.sum(grad_act * grad_act, axis=1))
    row_norms = jnp.sqrt(input_square * grad_square)
    clip_level = clip_share * jnp.sum(row_norms * live_mask) / live_count.astype(jnp.float32)
    factor = live_mask * jnp.minimum(1.0, clip_level / (row_norms + 1e-06))
    scaled = (grad_act * factor[:, None]).astype(jnp.bfloat16)
    update = jnp.dot(inputs.T, scaled, preferred_element_type=jnp.float32) + noise_scale * clip_level * noise_block.astype(jnp.float32)
    spread = jnp.mean(update * update)
    renewed = (weights.astype(jnp.float32) - learn_rate * update * lax.rsqrt(spread + 1e-06)).astype(jnp.bfloat16)
    return (renewed, losses)

def reference(tokens, targets, w_in, w_out, noise_field, step_size, clip_ratio, noise_mult, plan, live_rows):
    split_tokens = tokens.reshape(3, CONFIGS, ROWS, D)
    split_targets = targets.reshape(2, CONFIGS, ROWS, D)

    def round_step(members):
        return train_round(members[0], members[1], members[2], members[3], members[4], members[5], members[6], members[7], w_out)
    trained_one, loss_one = lax.map(round_step, (w_in, split_tokens[0], split_targets[0], noise_field, live_rows[0], step_size, clip_ratio, noise_mult))
    indices = jnp.arange(CONFIGS, dtype=jnp.int32)
    owners = lax.optimization_barrier(jnp.sum(indices[:, None] * (plan[:, None] == indices[None, :]).astype(jnp.int32), axis=0)).astype(jnp.int32)
    arrived = jnp.take(trained_one, owners, axis=0)
    trained_two, loss_two = lax.map(round_step, (arrived, split_tokens[1], split_targets[1], noise_field, live_rows[1], jnp.take(step_size, owners), jnp.take(clip_ratio, owners), jnp.take(noise_mult, owners)))

    def evaluate(members):
        pre_act = jnp.dot(members[1], members[0], preferred_element_type=jnp.float32)
        output, slope_value = gelu_parts(pre_act)
        return jnp.dot(output.astype(jnp.bfloat16), w_out, preferred_element_type=jnp.float32).astype(jnp.bfloat16)
    predictions = lax.map(evaluate, (trained_two, split_tokens[2])).reshape(CONFIGS * ROWS, D)
    row_losses = jnp.stack([loss_one.reshape(-1), loss_two.reshape(-1)])
    return (predictions, row_losses)
```

```python
import jax
import jax.numpy as jnp
from jax import lax
from jax.experimental import pallas as pl
from jax.experimental.pallas import tpu as pltpu
from jax.sharding import Mesh
from jax.sharding import PartitionSpec as P

D = 1024
FF = 32768
F32 = jnp.float32
BF16 = jnp.bfloat16
SWAP = [(0, 1), (1, 0)]
TENSOR = ("x", "h", "c")
HOP = ("y", "l")
TILE = 512


def to_all(x, axis):
    size = lax.axis_size(axis)
    return lax.all_to_all(jnp.broadcast_to(x[None], (size, *x.shape)), axis, 0, 0, tiled=True)


def each_its_own(x, axis):
    return lax.all_to_all(x, axis, 0, 0, tiled=True)


def swapped(x, axis):
    return lax.ppermute(x, axis, SWAP)


def turned(pieces, axis):
    return [pieces[0]] + [
        lax.ppermute(pieces[s], axis, [(i, (i + s) % 4) for i in range(4)]) for s in (1, 2, 3)
    ]


def in_order(own, other, index, axis):
    first = jnp.where(index == 0, own, other)
    second = jnp.where(index == 0, other, own)
    return jnp.stack([first, second], axis=axis)


def pick(x, index):
    return lax.dynamic_index_in_dim(x, index, 0, keepdims=False)


def gelu_parts(pre_act):
    inside = 0.7978845608 * (pre_act + 0.044715 * pre_act * pre_act * pre_act)
    tangent = jnp.tanh(inside)
    output = 0.5 * pre_act * (1.0 + tangent)
    slope_value = 0.5 * (1.0 + tangent) + 0.5 * pre_act * (
        1.0 - tangent * tangent
    ) * 0.7978845608 * (1.0 + 0.134145 * pre_act * pre_act)
    return (output, slope_value)


def dot(a, b, contract):
    return lax.dot_general(a, b, ((contract[:1], contract[1:]), ((), ())), preferred_element_type=F32)


def whole(*shape):
    return pl.BlockSpec(shape, lambda i: (0,) * len(shape))


def tiled_over(rows):
    return pl.BlockSpec((rows, TILE), lambda i: (0, i))


SCALARS = pl.BlockSpec(memory_space=pltpu.SMEM)


def add_product(active, columns, total):
    product = dot(active, columns, (1, 1))
    for k in range(8):
        total[k] += product[:, 128 * k : 128 * (k + 1)]


def hand_out(place_ref, total, own_ref, other_ref):
    even = place_ref[2] == 0
    for r in range(4):
        s = (place_ref[1] - r) & 3
        own_ref[s] = jnp.where(even, total[2 * r], total[2 * r + 1])
        other_ref[s] = jnp.where(even, total[2 * r + 1], total[2 * r])


def forward_body(base_ref, step_ref, square_ref, far_square_ref, place_ref, share_ref, columns_ref, *outs):
    own_ref, other_ref, rate_ref = outs[:3]
    total = outs[-1]

    @pl.when(pl.program_id(0) == 0)
    def _():
        total[...] = jnp.zeros_like(total)
        spread = jnp.maximum(square_ref[...] + far_square_ref[...], 0.0) / (D * FF)
        rate_ref[...] = share_ref[place_ref[0]] * lax.rsqrt(spread + 1e-06)

    pre = base_ref[...] - rate_ref[0:1, 0:1] * step_ref[...]
    output, slope = gelu_parts(pre)
    if len(outs) > 4:
        outs[3][...] = slope
    add_product(output.astype(BF16), columns_ref[...], total)

    @pl.when(pl.program_id(0) == pl.num_programs(0) - 1)
    def _():
        hand_out(place_ref, total, own_ref, other_ref)


def forward_step(base, step, squares, place, learn_rate, columns, with_slope):
    rows, width = base.shape
    block = jax.ShapeDtypeStruct((4, rows, 128), F32)
    shapes = [block, block, jax.ShapeDtypeStruct((1, 128), F32)]
    specs = [whole(4, rows, 128), whole(4, rows, 128), whole(1, 128)]
    if with_slope:
        shapes.append(jax.ShapeDtypeStruct((rows, width), F32))
        specs.append(tiled_over(rows))
    return pl.pallas_call(
        forward_body,
        grid=(width // TILE,),
        in_specs=[
            tiled_over(rows), tiled_over(rows), whole(1, 128), whole(1, 128), SCALARS, SCALARS,
            tiled_over(1024),
        ],
        out_specs=specs,
        out_shape=shapes,
        scratch_shapes=[pltpu.VMEM((8, rows, 128), F32)],
    )(base, step, *squares, place, learn_rate, columns)


def first_body(active_ref, place_ref, *refs):
    pieces, (columns_ref, own_ref, other_ref, total) = refs[:-4], refs[-4:]

    @pl.when(pl.program_id(0) == 0)
    def _():
        total[...] = jnp.zeros_like(total)

    at = 0
    for piece in pieces:
        size = piece.shape[0]
        columns_ref[at : at + size] = piece[...]
        at += size
    add_product(active_ref[...], columns_ref[...], total)

    @pl.when(pl.program_id(0) == pl.num_programs(0) - 1)
    def _():
        hand_out(place_ref, total, own_ref, other_ref)


def first_step(active, place, pieces):
    rows, width = active.shape
    block = jax.ShapeDtypeStruct((4, rows, 128), F32)
    return pl.pallas_call(
        first_body,
        grid=(width // TILE,),
        in_specs=[tiled_over(rows), SCALARS, *[tiled_over(p.shape[0]) for p in pieces]],
        out_specs=[tiled_over(1024), whole(4, rows, 128), whole(4, rows, 128)],
        out_shape=[jax.ShapeDtypeStruct((1024, width), BF16), block, block],
        scratch_shapes=[pltpu.VMEM((8, rows, 128), F32)],
    )(active, place, *pieces)


def noise_body(inputs_ref, noise_ref, first_ref, second_ref, third_ref, square_ref, total):
    step = pl.program_id(0)
    rows = first_ref.shape[0]

    @pl.when(step == 0)
    def _():
        total[...] = jnp.zeros_like(total)

    noise = noise_ref[...]
    product = dot(inputs_ref[...], noise, (1, 0))
    first_ref[...] = product[:rows]
    second_ref[...] = product[rows : 2 * rows].astype(BF16)
    third_ref[...] = product[2 * rows :].astype(BF16)
    wide = noise.astype(F32)
    total[...] += folded(jnp.sum((wide * wide).reshape(-1, 8, TILE), axis=0))

    @pl.when(step == pl.num_programs(0) - 1)
    def _():
        square_ref[...] = jnp.broadcast_to(jnp.sum(total[...], keepdims=True), (1, 128))


def noise_step(inputs, noise, rows):
    width = noise.shape[1]
    return pl.pallas_call(
        noise_body,
        grid=(width // TILE,),
        in_specs=[whole(*inputs.shape), tiled_over(1024)],
        out_specs=[*[tiled_over(rows)] * 3, whole(1, 128)],
        out_shape=[
            jax.ShapeDtypeStruct((rows, width), F32),
            jax.ShapeDtypeStruct((rows, width), BF16),
            jax.ShapeDtypeStruct((rows, width), BF16),
            jax.ShapeDtypeStruct((1, 128), F32),
        ],
        scratch_shapes=[pltpu.VMEM((8, 128), F32)],
    )(inputs, noise)


def on_diagonal(size):
    return lax.broadcasted_iota(jnp.int32, (size, size), 0) == lax.broadcasted_iota(
        jnp.int32, (size, size), 1
    )


def as_row(column):
    size = column.shape[0]
    return jnp.sum(jnp.where(on_diagonal(size), column, 0.0), axis=0, keepdims=True)


def folded(x):
    total = x[:, :128]
    for k in range(1, x.shape[1] // 128):
        total = total + x[:, 128 * k : 128 * (k + 1)]
    return total


def backward_body(
    own_0, own_1, own_2, own_3, other_0, other_1, other_2, other_3, place_ref,
    slope_ref, noise_ref, loss_ref, columns_ref,
    grad_ref, news_ref, lost_ref, cross_ref, gram_ref, backed, square_sum, cross_sum,
):
    step = pl.program_id(0)

    @pl.when(step == 0)
    def _():
        parts = ((own_0, own_1, own_2, own_3), (other_0, other_1, other_2, other_3))
        for q, parts_of in enumerate(parts):
            for k, part in enumerate(parts_of):
                at = 2 * ((place_ref[1] - k) & 3) + (place_ref[2] ^ q)
                backed[:, pl.ds(pl.multiple_of(128 * at, 128), 128)] = part[...]
        square_sum[...] = jnp.zeros_like(square_sum)
        cross_sum[...] = jnp.zeros_like(cross_sum)
        gram_ref[...] = jnp.zeros_like(gram_ref)

    grad = dot(backed[...], columns_ref[...], (1, 0)) * slope_ref[...]
    square_sum[...] += folded(grad * grad)
    cross_sum[...] += folded(grad * noise_ref[...].astype(F32))
    rounded = grad.astype(BF16)
    grad_ref[...] = rounded
    gram_ref[...] += dot(rounded, rounded, (1, 1))

    @pl.when(step == pl.num_programs(0) - 1)
    def _():
        news_ref[...] = as_row(jnp.sum(square_sum[...], axis=1, keepdims=True))
        lost_ref[...] = as_row(jnp.sum(loss_ref[...], axis=1, keepdims=True))
        cross_ref[...] = as_row(jnp.sum(cross_sum[...], axis=1, keepdims=True))


def backward_step(own, other, place, slope, noise_product, loss, columns):
    rows, width = slope.shape
    return pl.pallas_call(
        backward_body,
        grid=(width // TILE,),
        in_specs=[
            *[whole(rows, 128)] * 8, SCALARS, tiled_over(rows), tiled_over(rows),
            whole(rows, 128), tiled_over(1024),
        ],
        out_specs=[tiled_over(rows), *[whole(1, rows)] * 3, whole(rows, rows)],
        out_shape=[
            jax.ShapeDtypeStruct((rows, width), BF16),
            *[jax.ShapeDtypeStruct((1, rows), F32)] * 3,
            jax.ShapeDtypeStruct((rows, rows), F32),
        ],
        scratch_shapes=[
            pltpu.VMEM((rows, 1024), BF16),
            pltpu.VMEM((rows, 128), F32),
            pltpu.VMEM((rows, 128), F32),
        ],
    )(*own, *other, place, slope, noise_product, loss, columns)


def clip_body(
    news_ref, far_news_ref, own_square_ref, cross_ref, gram_ref, inner_ref, facts_ref, place_ref,
    share_ref, noise_ref, factor_ref, scale_ref, square_ref,
):
    rows = own_square_ref.shape[1]
    news = news_ref[...] + far_news_ref[...]
    live, noise_square = facts_ref[0:1, 0:1], facts_ref[1:2, 0:1]
    clip_share, noise_scale = share_ref[place_ref[0]], noise_ref[place_ref[0]]
    index = lax.broadcasted_iota(jnp.int32, (1, rows), 1).astype(F32)
    live_mask = (index < live).astype(F32)
    row_norms = jnp.sqrt(own_square_ref[...] * news)
    clip_level = clip_share * jnp.sum(row_norms * live_mask, axis=1, keepdims=True) / live
    factor = live_mask * jnp.minimum(1.0, clip_level / (row_norms + 1e-06))
    scale = noise_scale * clip_level
    column = jnp.sum(jnp.where(on_diagonal(rows), factor, 0.0), axis=1, keepdims=True)
    weighed = jnp.sum(gram_ref[...] * inner_ref[...] * column, axis=0, keepdims=True)
    square = jnp.sum((weighed + 2.0 * scale * cross_ref[...]) * factor, axis=1, keepdims=True)
    square = square + scale * scale * noise_square
    factor_ref[...] = factor
    scale_ref[...] = jnp.broadcast_to(scale, (1, 128))
    square_ref[...] = jnp.broadcast_to(square, (1, 128))


def clip_step(news, own_square, cross, gram, inner, facts, place, shares, noises):
    rows = own_square.shape[1]
    return pl.pallas_call(
        clip_body,
        in_specs=[pl.BlockSpec(memory_space=pltpu.VMEM)] * 7 + [SCALARS] * 3,
        out_specs=[pl.BlockSpec(memory_space=pltpu.VMEM)] * 3,
        out_shape=[
            jax.ShapeDtypeStruct((1, rows), F32),
            jax.ShapeDtypeStruct((1, 128), F32),
            jax.ShapeDtypeStruct((1, 128), F32),
        ],
    )(*news, own_square, cross, gram, inner, facts, place, shares, noises)


def all_but_h(x):
    x = x + swapped(x, "c")
    x = sum(turned([x] * 4, "x"))
    return x, swapped(x, "h")


def features_joined(pair, x, c):
    along = jnp.stack(turned([pair] * 4, "x"))
    natural = (x - jnp.arange(4, dtype=jnp.int32)) & 3
    along = along.at[natural].get(mode="promise_in_bounds")
    full = in_order(along, swapped(along, "c"), c, 2)
    return full.reshape(-1, pair.shape[2])


def column_moved(line, wanted, y):
    sends = [line(wanted[(y + s) & 3] & 3) for s in range(4)]
    return pick(jnp.stack(turned(sends, "y")), (y - (wanted[y] >> 2)) & 3)


def hop_moved(block, source, y, l):
    line = jnp.stack(turned([block] * 4, "l"))
    wanted = source.reshape(4, 4)[:, l]
    return column_moved(lambda k: pick(line, (l - k) & 3), wanted, y)


def sent_by_plan(product, plan):
    met = each_its_own(product.reshape(16, -1, product.shape[1]), HOP)
    met = met.at[plan].get(mode="promise_in_bounds")
    return each_its_own(met, HOP).reshape(product.shape)


def column_pieces(w_out):
    line = turned([w_out.T] * 4, "l")
    near = turned([line[0]] * 4, "y")
    rest = turned([jnp.concatenate([line[2], line[1], line[3]])] * 4, "y")
    return [part for r in range(4) for part in (near[r], rest[r])]


def in_turned_order(pair, flip, axis):
    return jnp.where(flip == 0, pair, jnp.flip(pair, axis))


def local(
    tokens, targets, w_in, w_out, noise_field, step_size, clip_ratio, noise_mult, plan, live_rows
):
    x, y, l, h, c = (lax.axis_index(a) for a in ("x", "y", "l", "h", "c"))
    me = 4 * y + l
    rows = tokens.shape[1]
    weights, noise = w_in[0], noise_field[0]
    indices = jnp.arange(plan.shape[0], dtype=jnp.int32)
    owners = jnp.sum(
        indices[:, None] * (plan[:, None] == indices[None, :]).astype(jnp.int32), axis=0
    )

    parity = (l + c) & 1
    flip = jnp.where(parity == 0, l, (l - 1) & 3) >> 1
    spot = jnp.arange(3, dtype=jnp.int32)
    place = jnp.where(spot == 0, me, jnp.where(spot == 1, (y - x) & 3, parity))

    pieces = column_pieces(w_out)
    block = jnp.concatenate([tokens, targets]).transpose(2, 0, 1).reshape(64, 5 * rows)
    pair = in_order(block, swapped(block, "h"), h, 0)
    own = features_joined(pair[:, :, : 3 * rows], x, c).T
    one = own[:rows]

    def half_target(pair):
        return in_turned_order(pair, flip, 0).reshape(128, rows).T.astype(F32)

    target_one = half_target(pair[:, :, 3 * rows : 4 * rows])
    mail = jnp.concatenate([pair[:, :, rows : 3 * rows], pair[:, :, 4 * rows :]], axis=2)
    mail = hop_moved(mail, plan, y, l)
    moved = features_joined(mail[:, :, : 2 * rows], x, c).T
    two, three = moved[:rows], moved[rows:]
    target_two = half_target(mail[:, :, 2 * rows :])

    noise_one, product_two, product_three, noise_square = noise_step(own, noise, rows)
    live = jnp.broadcast_to(live_rows.astype(F32), (2, 128))
    facts_one = jnp.concatenate([live[:1], noise_square])
    facts_two = to_all(jnp.concatenate([live[1:], noise_square]), HOP)
    facts_two = pick(facts_two, plan[me])

    pre_one = dot(one, weights, (1, 0))
    output, slope_one = gelu_parts(pre_one)
    active_one = output.astype(BF16)
    product_two, product_three = (
        sent_by_plan(product, plan)
        for product in (product_two, product_three)
    )
    base_two = lax.optimization_barrier(dot(two, weights, (1, 0)))
    base_three = lax.optimization_barrier(dot(three, weights, (1, 0)))
    noise_two = lax.optimization_barrier(dot(two, noise, (1, 0)))
    noise_three = lax.optimization_barrier(dot(three, noise, (1, 0)))

    def chip_summed(own_part, other_part):
        chip = (own_part + swapped(other_part, "c")).astype(BF16)
        arrived = turned([chip[k] for k in range(4)], "x")
        return sum(part.astype(F32) for part in arrived)

    def train(own_part, other_part, slope, inputs, target, noise_product, facts):
        half = chip_summed(own_part, other_part)
        result = half + swapped(half.astype(BF16), "h").astype(F32)
        differ = result - target
        along = turned([differ.astype(BF16)] * 4, "x")
        along = [along[0], along[3], along[2], along[1]]
        grad, news, lost, cross, gram = backward_step(
            along, [swapped(part, "c") for part in along], place, slope, noise_product,
            0.25 * differ * differ, columns,
        )
        news = all_but_h(news)
        inner = dot(inputs, inputs, (1, 1))
        input_square = jnp.sum(jnp.square(inputs.astype(F32)), axis=1)[None, :]
        factor, scale, square = clip_step(
            news, input_square, cross, gram, inner, facts, place, clip_ratio, noise_mult
        )
        squares = all_but_h(square)
        return lost, grad, factor, scale[:, :1], squares

    def correction(inner, factor, grad, scale, noise_product):
        mixed = (inner * factor).astype(BF16)
        return dot(mixed, grad, (1, 0)) + scale * noise_product.astype(F32)

    columns, *parts = first_step(active_one, place, pieces)
    lost_one, grad_one, factor_one, scale_one, squares = train(
        *parts, slope_one, one, target_one, noise_one, facts_one
    )
    inner_two = dot(two, one, (1, 1))
    inner_three = dot(three, one, (1, 1))
    inner_last = dot(three, two, (1, 1))
    step_two = correction(inner_two, factor_one, grad_one, scale_one, noise_two)
    step_three = lax.optimization_barrier(
        correction(inner_three, factor_one, grad_one, scale_one, noise_three)
    )
    *parts, rate_one, slope_two = forward_step(
        base_two, step_two, squares, place, step_size, columns, True
    )
    lost_two, grad_two, factor_two, scale_two, squares = train(
        *parts, slope_two, two, target_two, product_two, facts_two
    )
    base_three = base_three - rate_one[:, :1] * step_three
    step_last = correction(inner_last, factor_two, grad_two, scale_two, product_three)
    losses = jnp.sum(to_all(jnp.concatenate([lost_one, lost_two]), TENSOR), axis=0)
    index = jnp.arange(rows, dtype=jnp.int32)
    losses = losses * jnp.stack([index < live_rows[0, 0], index < facts_two[0, 0].astype(jnp.int32)])
    second = pick(to_all(losses[1:], HOP), owners[me])
    *parts, _ = forward_step(base_three, step_last, squares, place, step_size, columns, False)
    half = chip_summed(*parts).astype(BF16).T.reshape(1, 2, 64, rows)
    half = in_turned_order(half, flip, 1)
    half = jnp.broadcast_to(half, (4, 2, 64, rows)).reshape(8, 64, rows)
    line = each_its_own(half, ("l", "h")).reshape(4, 2, 64, rows)
    line = jnp.sum(line.astype(F32), axis=1).astype(BF16)
    wanted = owners.reshape(4, 4)[:, l]
    answer = column_moved(lambda k: pick(line, k), wanted, y)
    return (answer.T, jnp.concatenate([losses[:1], second]))


def solution(mesh):
    fine = Mesh(mesh.devices.reshape(4, 4, 4, 2, 2), ("y", "l", "x", "h", "c"))

    return jax.shard_map(
        local,
        mesh=fine,
        in_specs=(
            P(None, HOP, TENSOR),
            P(None, HOP, TENSOR),
            P(HOP, None, TENSOR),
            P(TENSOR, HOP),
            P(HOP, None, TENSOR),
            P(),
            P(),
            P(),
            P(),
            P(None, HOP),
        ),
        out_specs=(P(HOP, TENSOR), P(None, HOP)),
        check_vma=False,
    )
```

```python
import functools

import jax
import jax.numpy as jnp
from jax import lax
from jax.experimental import pallas as pl
from jax.experimental.pallas import tpu as pltpu
from jax.sharding import Mesh
from jax.sharding import PartitionSpec as P

D = 1024
FF = 32768
F32 = jnp.float32
BF16 = jnp.bfloat16
SWAP = [(0, 1), (1, 0)]
TENSOR = ("x", "h", "c")
HOP = ("y", "l")
TILE = 1024


def each_its_own(x, axis):
    return lax.all_to_all(x, axis, 0, 0, tiled=True)


def swapped(x, axis):
    return lax.ppermute(x, axis, SWAP)


def turned(pieces, axis):
    return [pieces[0]] + [
        lax.ppermute(pieces[s], axis, [(i, (i + s) % 4) for i in range(4)]) for s in (1, 2, 3)
    ]


def in_order(own, other, index, axis):
    first = jnp.where(index == 0, own, other)
    second = jnp.where(index == 0, other, own)
    return jnp.stack([first, second], axis=axis)


def pick(x, index):
    return lax.dynamic_index_in_dim(x, index, 0, keepdims=False)


def gelu_parts(pre_act):
    inside = 0.7978845608 * (pre_act + 0.044715 * pre_act * pre_act * pre_act)
    tangent = jnp.tanh(inside)
    output = 0.5 * pre_act * (1.0 + tangent)
    slope_value = 0.5 * (1.0 + tangent) + 0.5 * pre_act * (
        1.0 - tangent * tangent
    ) * 0.7978845608 * (1.0 + 0.134145 * pre_act * pre_act)
    return (output, slope_value)


def dot(a, b, contract):
    return lax.dot_general(a, b, ((contract[:1], contract[1:]), ((), ())), preferred_element_type=F32)


def whole(*shape):
    return pl.BlockSpec(shape, lambda i: (0,) * len(shape))


def tiled_over(rows):
    return pl.BlockSpec((rows, TILE), lambda i: (0, i))


SCALARS = pl.BlockSpec(memory_space=pltpu.SMEM)


def add_product(active, columns, total):
    total[...] += dot(columns, active, (1, 1))


def hand_out(place_ref, total, own_ref, other_ref):
    even = place_ref[2] == 0
    for r in range(4):
        s = (place_ref[1] - r) & 3
        first, second = total[256 * r : 256 * r + 128], total[256 * r + 128 : 256 * r + 256]
        own_ref[s] = jnp.where(even, first, second)
        other_ref[s] = jnp.where(even, second, first)


def natural_sum(x, parts, scratch):
    for k, part in enumerate(parts):
        scratch[(x - k) & 3] = part[...]
    return scratch[0] + scratch[1] + scratch[2] + scratch[3]


def forward_body(terms, place_ref, share_ref, base_ref, columns_ref, *refs):
    steps, outs = refs[: 8 * terms], refs[8 * terms :]
    own_ref, other_ref = outs[:2]
    total, spread_parts = outs[-2:]

    @pl.when(pl.program_id(0) == 0)
    def _():
        total[...] = jnp.zeros_like(total)

    pre = base_ref[...]
    for k in range(terms):
        mixed_ref, grad_ref, noise_ref, scale_ref = steps[8 * k : 8 * k + 4]
        square = natural_sum(place_ref[3], steps[8 * k + 4 : 8 * k + 8], spread_parts)
        spread = jnp.maximum(square, 0.0) / (D * FF)
        rate = share_ref[place_ref[0]] * lax.rsqrt(spread + 1e-06)
        move = dot(mixed_ref[...], grad_ref[...], (1, 0))
        move = move + scale_ref[0:1, 0:1] * noise_ref[...].astype(F32)
        pre = pre - rate[0:1, 0:1] * move
    output, slope = gelu_parts(pre)
    if len(outs) > 4:
        outs[2][...] = slope
    add_product(output.astype(BF16), columns_ref[...], total)

    @pl.when(pl.program_id(0) == pl.num_programs(0) - 1)
    def _():
        hand_out(place_ref, total, own_ref, other_ref)


def forward_step(base, steps, place, learn_rate, columns, with_slope):
    rows, width = base.shape
    shapes = [jax.ShapeDtypeStruct((4, 128, rows), F32)] * 2
    specs = [whole(4, 128, rows)] * 2
    if with_slope:
        shapes.append(jax.ShapeDtypeStruct((rows, width), F32))
        specs.append(tiled_over(rows))
    step_specs = [whole(rows, rows), tiled_over(rows), tiled_over(rows), *[whole(1, 128)] * 5]
    return pl.pallas_call(
        functools.partial(forward_body, len(steps)),
        grid=(width // TILE,),
        in_specs=[SCALARS, SCALARS, tiled_over(rows), tiled_over(1024), *step_specs * len(steps)],
        out_specs=specs,
        out_shape=shapes,
        scratch_shapes=[pltpu.VMEM((1024, rows), F32), pltpu.VMEM((4, 1, 128), F32)],
    )(place, learn_rate, base, columns, *[part for step in steps for part in step])


def first_body(active_ref, place_ref, *refs):
    pieces, (columns_ref, own_ref, other_ref, total) = refs[:-4], refs[-4:]

    @pl.when(pl.program_id(0) == 0)
    def _():
        total[...] = jnp.zeros_like(total)

    at = 0
    for piece in pieces:
        size = piece.shape[0]
        columns_ref[at : at + size] = piece[...]
        at += size
    add_product(active_ref[...], columns_ref[...], total)

    @pl.when(pl.program_id(0) == pl.num_programs(0) - 1)
    def _():
        hand_out(place_ref, total, own_ref, other_ref)


def first_step(active, place, pieces):
    rows, width = active.shape
    block = jax.ShapeDtypeStruct((4, 128, rows), F32)
    return pl.pallas_call(
        first_body,
        grid=(width // TILE,),
        in_specs=[tiled_over(rows), SCALARS, *[tiled_over(p.shape[0]) for p in pieces]],
        out_specs=[tiled_over(1024), whole(4, 128, rows), whole(4, 128, rows)],
        out_shape=[jax.ShapeDtypeStruct((1024, width), BF16), block, block],
        scratch_shapes=[pltpu.VMEM((1024, rows), F32)],
    )(active, place, *pieces)


def base_body(inputs_ref, weights_ref, noise_ref, base_ref, product_ref):
    base_ref[...] = dot(inputs_ref[...], weights_ref[...], (1, 0))
    product_ref[...] = dot(inputs_ref[...], noise_ref[...], (1, 0)).astype(BF16)


def base_step(inputs, weights, noise):
    rows, width = inputs.shape[0], noise.shape[1]
    return pl.pallas_call(
        base_body,
        grid=(width // TILE,),
        in_specs=[whole(*inputs.shape), tiled_over(1024), tiled_over(1024)],
        out_specs=[tiled_over(rows)] * 2,
        out_shape=[
            jax.ShapeDtypeStruct((rows, width), F32),
            jax.ShapeDtypeStruct((rows, width), BF16),
        ],
    )(inputs, weights, noise)


def noise_body(inputs_ref, noise_ref, first_ref, second_ref, third_ref):
    rows = first_ref.shape[0]
    product = dot(inputs_ref[...], noise_ref[...], (1, 0)).astype(BF16)
    first_ref[...] = product[:rows]
    second_ref[...] = product[rows : 2 * rows]
    third_ref[...] = product[2 * rows :]


def noise_step(inputs, noise, rows):
    width = noise.shape[1]
    return pl.pallas_call(
        noise_body,
        grid=(width // TILE,),
        in_specs=[whole(*inputs.shape), tiled_over(1024)],
        out_specs=[tiled_over(rows)] * 3,
        out_shape=[jax.ShapeDtypeStruct((rows, width), BF16)] * 3,
    )(inputs, noise)


def on_diagonal(size):
    return lax.broadcasted_iota(jnp.int32, (size, size), 0) == lax.broadcasted_iota(
        jnp.int32, (size, size), 1
    )


def as_row(column):
    size = column.shape[0]
    return jnp.sum(jnp.where(on_diagonal(size), column, 0.0), axis=0, keepdims=True)


def folded(x):
    total = x[:, :128]
    for k in range(1, x.shape[1] // 128):
        total = total + x[:, 128 * k : 128 * (k + 1)]
    return total


def backward_body(
    part_0, part_1, part_2, part_3, place_ref, slope_ref, noise_ref, loss_ref, columns_ref,
    grad_ref, news_ref, cross_ref, gram_ref, backed, square_sum, cross_sum,
):
    step = pl.program_id(0)
    rows = slope_ref.shape[0]

    @pl.when(step == 0)
    def _():
        for k, part in enumerate((part_0, part_1, part_2, part_3)):
            for q in range(2):
                at = 2 * ((place_ref[1] - k) & 3) + (place_ref[2] ^ q)
                turned_part = part[q].astype(F32).T.astype(BF16)
                backed[:, pl.ds(pl.multiple_of(128 * at, 128), 128)] = turned_part
        square_sum[...] = jnp.zeros_like(square_sum)
        cross_sum[...] = jnp.zeros_like(cross_sum)
        gram_ref[...] = jnp.zeros_like(gram_ref)

    grad = dot(backed[...], columns_ref[...], (1, 0)) * slope_ref[...]
    square_sum[...] += folded(grad * grad)
    cross_sum[...] += folded(grad * noise_ref[...].astype(F32))
    rounded = grad.astype(BF16)
    grad_ref[...] = rounded
    gram_ref[...] += dot(rounded, rounded, (1, 1))

    @pl.when(step == pl.num_programs(0) - 1)
    def _():
        news_ref[:, :rows] = as_row(jnp.sum(square_sum[...], axis=1, keepdims=True))
        news_ref[:, rows:] = jnp.sum(loss_ref[...], axis=0, keepdims=True)
        cross_ref[...] = as_row(jnp.sum(cross_sum[...], axis=1, keepdims=True))


def backward_step(parts, place, slope, noise_product, loss, columns):
    rows, width = slope.shape
    return pl.pallas_call(
        backward_body,
        grid=(width // TILE,),
        in_specs=[
            *[whole(2, 128, rows)] * 4, SCALARS, tiled_over(rows), tiled_over(rows),
            whole(128, rows), tiled_over(1024),
        ],
        out_specs=[tiled_over(rows), whole(1, 2 * rows), whole(1, rows), whole(rows, rows)],
        out_shape=[
            jax.ShapeDtypeStruct((rows, width), BF16),
            jax.ShapeDtypeStruct((1, 2 * rows), F32),
            jax.ShapeDtypeStruct((1, rows), F32),
            jax.ShapeDtypeStruct((rows, rows), F32),
        ],
        scratch_shapes=[
            pltpu.VMEM((rows, 1024), BF16),
            pltpu.VMEM((rows, 128), F32),
            pltpu.VMEM((rows, 128), F32),
        ],
    )(*parts, place, slope, noise_product, loss, columns)


def clip_body(
    news_0, news_1, news_2, news_3, own_square_ref, cross_ref, gram_ref, inner_ref, facts_ref,
    place_ref, share_ref, noise_ref, *refs,
):
    rows = own_square_ref.shape[1]
    *others, loss_ref, scale_ref, square_ref, parts = refs
    news = natural_sum(place_ref[3], (news_0, news_1, news_2, news_3), parts)
    live, noise_square = facts_ref[0:1, 0:1], facts_ref[1:2, 0:1]
    clip_share, noise_scale = share_ref[place_ref[0]], noise_ref[place_ref[0]]
    index = lax.broadcasted_iota(jnp.int32, (1, rows), 1).astype(F32)
    live_mask = (index < live).astype(F32)
    row_norms = jnp.sqrt(own_square_ref[...] * news[:, :rows])
    clip_level = clip_share * jnp.sum(row_norms * live_mask, axis=1, keepdims=True) / live
    factor = live_mask * jnp.minimum(1.0, clip_level / (row_norms + 1e-06))
    scale = noise_scale * clip_level
    column = jnp.sum(jnp.where(on_diagonal(rows), factor, 0.0), axis=1, keepdims=True)
    weighed = jnp.sum(gram_ref[...] * inner_ref[...] * column, axis=0, keepdims=True)
    square = jnp.sum((weighed + 2.0 * scale * cross_ref[...]) * factor, axis=1, keepdims=True)
    square = square + scale * scale * noise_square
    half = len(others) // 2
    for other_ref, mixed_ref in zip(others[:half], others[half:]):
        mixed_ref[...] = (other_ref[...] * factor).astype(BF16)
    loss_ref[...] = news[:, rows:] * live_mask
    scale_ref[...] = jnp.broadcast_to(scale, (1, 128))
    square_ref[...] = jnp.broadcast_to(square, (1, 128))


def clip_step(news, own_square, cross, gram, inner, facts, place, shares, noises, others):
    rows = own_square.shape[1]
    vmem = pl.BlockSpec(memory_space=pltpu.VMEM)
    return pl.pallas_call(
        clip_body,
        in_specs=[vmem] * 9 + [SCALARS] * 3 + [vmem] * len(others),
        out_specs=[vmem] * (len(others) + 3),
        out_shape=[
            *[jax.ShapeDtypeStruct((rows, rows), BF16)] * len(others),
            jax.ShapeDtypeStruct((1, rows), F32),
            jax.ShapeDtypeStruct((1, 128), F32),
            jax.ShapeDtypeStruct((1, 128), F32),
        ],
        scratch_shapes=[pltpu.VMEM((4, 1, 2 * rows), F32)],
    )(*news, own_square, cross, gram, inner, facts, place, shares, noises, *others)


def all_but_x(x):
    x = x + swapped(x, "c")
    x = x + swapped(x, "h")
    return turned([x] * 4, "x")


def features_joined(pair, x, c):
    along = jnp.stack(turned([pair] * 4, "x"))
    natural = (x - jnp.arange(4, dtype=jnp.int32)) & 3
    along = along.at[natural].get(mode="promise_in_bounds")
    other = swapped(along, "c")
    return in_order(along, other, c, 2).reshape(-1, pair.shape[2]).T


def column_moved(line, wanted, y):
    sends = [line(wanted[(y + s) & 3] & 3) for s in range(4)]
    return pick(jnp.stack(turned(sends, "y")), (y - (wanted[y] >> 2)) & 3)


def hop_moved(block, source, y, l):
    line = jnp.stack(turned([block] * 4, "l"))
    wanted = source.reshape(4, 4)[:, l]
    return column_moved(lambda k: pick(line, (l - k) & 3), wanted, y)


def sent_by_plan(product, plan):
    met = each_its_own(product.reshape(16, -1, product.shape[1]), HOP)
    met = met.at[plan].get(mode="promise_in_bounds")
    return each_its_own(met, HOP).reshape(product.shape)


def column_pieces(w_out):
    line = turned([w_out.T] * 4, "l")
    near = turned([line[0]] * 4, "y")
    rest = turned([jnp.concatenate([line[2], line[1], line[3]])] * 4, "y")
    return [part for r in range(4) for part in (near[r], rest[r])]


def in_turned_order(pair, flip, axis):
    return jnp.where(flip == 0, pair, jnp.flip(pair, axis))


def local(
    tokens, targets, w_in, w_out, noise_field, step_size, clip_ratio, noise_mult, plan, live_rows
):
    x, y, l, h, c = (lax.axis_index(a) for a in ("x", "y", "l", "h", "c"))
    me = 4 * y + l
    rows = tokens.shape[1]
    weights, noise = w_in[0], noise_field[0]
    indices = jnp.arange(plan.shape[0], dtype=jnp.int32)
    owners = jnp.sum(
        indices[:, None] * (plan[:, None] == indices[None, :]).astype(jnp.int32), axis=0
    )

    parity = (l + c) & 1
    flip = jnp.where(parity == 0, l, (l - 1) & 3) >> 1
    spot = jnp.arange(4, dtype=jnp.int32)
    place = jnp.where(spot == 0, me, jnp.where(spot == 1, (y - x) & 3, jnp.where(spot == 2, parity, x)))

    pieces = column_pieces(w_out)
    block = jnp.concatenate([tokens, targets]).transpose(2, 0, 1).reshape(64, 5 * rows)
    pair = in_order(block, swapped(block, "h"), h, 0)
    own = features_joined(pair[:, :, : 3 * rows], x, c)
    one = own[:rows]

    def half_target(pair):
        return in_turned_order(pair, flip, 0).reshape(128, rows).astype(F32)

    target_one = half_target(pair[:, :, 3 * rows : 4 * rows])
    square = jnp.sum(jnp.square(noise.astype(F32)))
    live = live_rows.astype(F32)
    high = lax.reduce_precision(square, 8, 7)
    middle = lax.reduce_precision(square - high, 8, 7)
    row = lax.broadcasted_iota(jnp.int32, (2, 64, 128), 1)
    facts = jnp.where(row == 0, live[1, 0], jnp.where(row == 1, high, jnp.where(row == 2, middle, square - high - middle)))
    mail = jnp.concatenate(
        [pair[:, :, rows : 3 * rows], pair[:, :, 4 * rows :], facts.astype(BF16)], axis=2
    )
    mail = hop_moved(mail, plan, y, l)
    moved = features_joined(mail[:, :, : 2 * rows], x, c)
    two, three = moved[:rows], moved[rows:]
    target_two = half_target(mail[:, :, 2 * rows : 3 * rows])
    facts_one = jnp.broadcast_to(jnp.stack([live[0, 0], square])[:, None], (2, 128))
    facts_two = mail[0, :4, 3 * rows :].astype(F32)
    facts_two = jnp.stack([facts_two[0], facts_two[1] + facts_two[2] + facts_two[3]])

    noise_one, product_two, product_three = noise_step(own, noise, rows)

    pre_one = dot(one, weights, (1, 0))
    output, slope_one = gelu_parts(pre_one)
    active_one = output.astype(BF16)
    product_two, product_three = (
        sent_by_plan(product, plan)
        for product in (product_two, product_three)
    )
    base_two, noise_two = base_step(two, weights, noise)
    base_three, noise_three = base_step(three, weights, noise)

    def chip_summed(own_part, other_part):
        chip = (own_part + swapped(other_part, "c")).astype(BF16)
        arrived = turned([chip[k] for k in range(4)], "x")
        return sum(part.astype(F32) for part in arrived)

    def train(parts, slope, inputs, target, noise_product, facts, others):
        half = chip_summed(*parts)
        far = swapped(half.astype(BF16), "h")
        result = half + far.astype(F32)
        differ = result - target
        backed = differ.astype(BF16)
        loss_part = 0.25 * differ * differ
        backed = jnp.stack([backed, swapped(backed, "c")])
        along = turned([backed] * 4, "x")
        grad, news, cross, gram = backward_step(
            [along[0], along[3], along[2], along[1]], place, slope, noise_product,
            loss_part, columns,
        )
        news = all_but_x(news)
        inner = dot(inputs, inputs, (1, 1))
        input_square = jnp.sum(jnp.square(inputs.astype(F32)), axis=1)[None, :]
        others = [dot(other, inputs, (1, 1)) for other in others]
        *mixed, loss, scale, square = clip_step(
            news, input_square, cross, gram, inner, facts, place, clip_ratio, noise_mult, others,
        )
        squares = all_but_x(square)
        return loss, [(each, grad, scale, squares) for each in mixed]

    def with_noise(step, noise_product):
        mixed, grad, scale, squares = step
        return (mixed, grad, noise_product, scale, *squares)

    columns, *parts = first_step(active_one, place, pieces)
    loss_one, (step_two, step_three) = train(
        parts, slope_one, one, target_one, noise_one, facts_one, (two, three)
    )
    *parts, slope_two = forward_step(
        base_two, [with_noise(step_two, noise_two)], place, step_size, columns, True
    )
    loss_two, (step_last,) = train(
        parts, slope_two, two, target_two, product_two, facts_two, (three,)
    )
    steps = [with_noise(step_three, noise_three), with_noise(step_last, product_three)]
    parts = forward_step(base_three, steps, place, step_size, columns, False)
    half = chip_summed(*parts).astype(BF16).reshape(2, 64, rows)
    half = in_turned_order(half, flip, 0)
    high = lax.reduce_precision(loss_two, 8, 7)
    tail = jnp.concatenate([high, loss_two - high, jnp.zeros((14, rows), F32)]).astype(BF16)
    half = jnp.concatenate([half, jnp.broadcast_to(tail, (2, 16, rows))], axis=1)
    half = jnp.broadcast_to(half, (4, *half.shape)).reshape(8, 80, rows)
    line = each_its_own(half, ("l", "h")).reshape(4, 2, 80, rows)
    line = jnp.sum(line.astype(F32), axis=1).astype(BF16)
    wanted = owners.reshape(4, 4)[:, l]
    answer = column_moved(lambda k: pick(line, k), wanted, y)
    second = 0.5 * jnp.sum(answer[64:66].astype(F32), axis=0, keepdims=True)
    return (answer[:64].T, jnp.concatenate([loss_one, second]))


def solution(mesh):
    fine = Mesh(mesh.devices.reshape(4, 4, 4, 2, 2), ("y", "l", "x", "h", "c"))

    return jax.shard_map(
        local,
        mesh=fine,
        in_specs=(
            P(None, HOP, TENSOR),
            P(None, HOP, TENSOR),
            P(HOP, None, TENSOR),
            P(TENSOR, HOP),
            P(HOP, None, TENSOR),
            P(),
            P(),
            P(),
            P(),
            P(None, HOP),
        ),
        out_specs=(P(HOP, TENSOR), P(None, HOP)),
        check_vma=False,
    )
```
